32 devices in a mesh: dp: 16 (over z, x, core), tensor: 2 (over y).
Axes of the slice: x: 2, y: 2, z: 4, core: 2. Of those that a mesh axis runs over, the one named last changes fastest.
Arguments:
- tokens: bfloat16 [16384, 1024], P(('dp', 'tensor')), may hold values from -6 to 6
- cotangent: bfloat16 [16384, 1024], P(('dp', 'tensor')), may hold values from -6 to 6
- starts: int32 [16384], P('dp'), may hold values from 0 to 1023, as said below
- first_gain: bfloat16 [1024], P('dp'), may hold values from 0.5 to 1.5
- first_shift: bfloat16 [1024], P('dp'), may hold values from -3 to 3
- attention: bfloat16 [3, 1024, 1024], P(None, 'dp', 'tensor'), may hold values from -0.1875 to 0.1875
- attention_bias: bfloat16 [2, 16, 64], P(None, 'tensor', 'dp'), may hold values from -2 to 2
- combine: bfloat16 [1024, 1024], P('tensor', 'dp'), may hold values from -1.5 to 1.5
- combine_bias: bfloat16 [1024], P('dp'), may hold values from -3 to 3
- second_gain: bfloat16 [1024], P('dp'), may hold values from 0.5 to 1.5
- second_shift: bfloat16 [1024], P('dp'), may hold values from -3 to 3
- expand: bfloat16 [1024, 4096], P('dp', 'tensor'), may hold values from -0.1875 to 0.1875
- expand_bias: bfloat16 [16, 256], P('tensor', 'dp'), may hold values from -3 to 3
- contract: bfloat16 [4096, 1024], P('tensor', 'dp'), may hold values from -0.09375 to 0.09375
- contract_bias: bfloat16 [1024], P('dp'), may hold values from -4 to 4
Outputs:
- result: float32 [16384, 1024], P(('dp', 'tensor'))
- tokens_grad: float32 [16384, 1024], P(('dp', 'tensor'))
- firstgain_grad: float32 [1024], P(('dp', 'tensor'))
- firstshift_grad: float32 [1024], P(('dp', 'tensor'))
- attention_grad: float32 [3, 1024, 1024], P(None, 'dp', 'tensor')
- attenbias_grad: float32 [2, 16, 64], P(None, 'tensor', 'dp')
- combine_grad: float32 [1024, 1024], P('tensor', 'dp')
- combias_grad: float32 [1024], P(('dp', 'tensor'))
- secondgain_grad: float32 [1024], P(('dp', 'tensor'))
- secondshift_grad: float32 [1024], P(('dp', 'tensor'))
- expand_grad: float32 [1024, 4096], P('dp', 'tensor')
- expbias_grad: float32 [16, 256], P('tensor', 'dp')
- contract_grad: float32 [4096, 1024], P('tensor', 'dp')
- conbias_grad: float32 [1024], P(('dp', 'tensor'))
The draws below stay inside these ranges and needn't reach their ends.
Inputs may be any that keep to these rules, and one draw needn't show every extreme that they name: Each group's 1024 tokens form consecutive sequences, so no sequence crosses a group's border, and at the first token of each sequence starts equals that token's own position within its group. In every draw some group holds one sequence of all 1024 tokens, and some other group ends with a sequence of one token.
All inputs are finite; a program needn't handle non-finite values.
Results may differ from the reference program's by a relative error of at most 0.02.
Values may be sent and summed in bfloat16 or wider, within the bound.
A program may use at most 256 MiB of HBM per device.

```python
import math
import jax
import jax.numpy as jnp
from jax import lax

D = 1024
H = 16
HD = 64
FF = 4096
TOK_G = 1024
TOKENS = 16384


def draw_starts(key, part):
    groups = TOKENS // TOK_G
    level_key, pick_key, roll_key, other_key = jax.random.split(key, 4)
    levels = jax.random.randint(level_key, (groups,), 0, 4)
    single = jax.random.randint(pick_key, (), 0, groups)
    other = (single + 1 + jax.random.randint(other_key, (), 0, groups - 1)) % groups
    group_index = jnp.arange(groups, dtype=jnp.int32)
    levels = jnp.where(group_index == single, 0, levels)
    limits = jnp.array([0, 2, 8, 32], jnp.int32)
    cutoff = jnp.sum(jnp.where(levels[:, None] == jnp.arange(4)[None, :], limits[None, :], 0), axis=1)
    dice_rolls = jax.random.randint(roll_key, (groups, TOK_G), 0, 1024)
    position = jnp.arange(TOK_G, dtype=jnp.int32)
    breaks = (dice_rolls < cutoff[:, None]) | (position[None, :] == 0)
    breaks = breaks | (group_index[:, None] == other) & (position[None, :] == TOK_G - 1)
    break_marks = jnp.where(breaks, position[None, :], 0)
    return lax.cummax(break_marks, axis=1).reshape(TOKENS).astype(jnp.int32)


def draw_attention_bias(key, part):
    sample = jnp.clip(jax.random.normal(key, (2, H, HD), jnp.float32), -4.0, 4.0)
    return (sample * 0.5).astype(jnp.bfloat16)


def level_of(key, extent, cuts, least, top_value):
    loudness = 1.0
    for dim, parts in cuts:
        draws = jax.random.uniform(jax.random.fold_in(jax.random.fold_in(key, 6), dim), (parts,), jnp.float32, least / len(cuts), top_value / len(cuts))
        loudness = loudness * jnp.repeat(jnp.exp(draws), extent[dim] // parts).reshape((-1,) + (1,) * (len(extent) - 1 - dim))
    return loudness


def noise(own_key, shape, width, reach, shards=(), held_as=jnp.bfloat16):
    result = width * jax.random.normal(own_key, shape, jnp.float32)
    if shards:
        result = result * level_of(own_key, shape, shards, -0.22, 0.18)
    return jnp.clip(result, -reach, reach).astype(held_as)


def setup_inputs(seed: int = 0) -> dict:
    splits = jax.random.split(jax.random.key(seed), 16)
    tokens = noise(splits[0], (TOKENS, D), 1.0, 6.0, ((0, 32),))
    cotangent = noise(splits[1], (TOKENS, D), 1.0, 6.0, ((0, 32),))
    starts = draw_starts(jax.random.fold_in(splits[15], 71), 0)
    first_gain = jnp.clip(1.0 + 0.1 * jax.random.normal(splits[3], (D,), jnp.float32), 0.5, 1.5).astype(jnp.bfloat16)
    first_shift = noise(splits[4], (D,), 0.3, 3.0, ((0, 16),))
    attention = noise(splits[5], (3, D, D), D ** -0.5, 0.1875, ((1, 16), (2, 2)))
    attention_bias = draw_attention_bias(jax.random.fold_in(splits[15], 71), 0)
    combine = noise(splits[7], (D, D), (HD // 4) ** -0.5, 1.5, ((0, 2), (1, 16)))
    combine_bias = noise(splits[8], (D,), 0.5, 3.0, ((0, 16),))
    second_gain = jnp.clip(1.0 + 0.1 * jax.random.normal(splits[9], (D,), jnp.float32), 0.5, 1.5).astype(jnp.bfloat16)
    second_shift = noise(splits[10], (D,), 0.3, 3.0, ((0, 16),))
    expand = noise(splits[11], (D, FF), D ** -0.5, 0.1875, ((0, 16), (1, 2)))
    expand_bias = noise(splits[12], (H, FF // H), 0.5, 3.0, ((0, 2), (1, 16)))
    contract = noise(splits[13], (FF, D), FF ** -0.5, 0.09375, ((0, 2), (1, 16)))
    contract_bias = noise(splits[14], (D,), 1.0, 4.0, ((0, 16),))
    return dict(tokens=tokens, cotangent=cotangent, starts=starts, first_gain=first_gain, first_shift=first_shift, attention=attention, attention_bias=attention_bias, combine=combine, combine_bias=combine_bias, second_gain=second_gain, second_shift=second_shift, expand=expand, expand_bias=expand_bias, contract=contract, contract_bias=contract_bias)


EPSILON = 1e-05
SQRT_TWO_PI = 0.7978845608028654
CUBIC = 0.044715
HIGHEST_PRECISION = lax.Precision.HIGHEST

def normalize(values):
    center = values - lax.optimization_barrier(jnp.mean(values, axis=-1, keepdims=True))
    inverse = lax.rsqrt(lax.optimization_barrier(jnp.mean(center * center, axis=-1, keepdims=True)) + EPSILON)
    return (center * inverse, inverse)

def normalize_back(upstream, unit_rows, inverse, gain):
    scaled = upstream * gain
    return inverse * (scaled - lax.optimization_barrier(jnp.mean(scaled, axis=-1, keepdims=True)) - unit_rows * lax.optimization_barrier(jnp.mean(scaled * unit_rows, axis=-1, keepdims=True)))

def gelu_tanh(hidden):
    return 0.5 * hidden * (1.0 + jnp.tanh(SQRT_TWO_PI * (hidden + CUBIC * hidden * hidden * hidden)))

def rounded(values):
    return lax.optimization_barrier(values.astype(jnp.bfloat16)).astype(jnp.float32)

def wide(values):
    return values.astype(jnp.float32)

def reference(tokens, cotangent, starts, first_gain, first_shift, attention, attention_bias, combine, combine_bias, second_gain, second_shift, expand, expand_bias, contract, contract_bias):
    groups = TOKENS // TOK_G
    gain_one = wide(first_gain)
    shift_one = wide(first_shift)
    gain_two = wide(second_gain)
    shift_two = wide(second_shift)
    bias_combine = wide(combine_bias)
    bias_contract = wide(contract_bias)
    query_bias = wide(attention_bias[0].reshape(D))
    value_bias = wide(attention_bias[1].reshape(D))
    hidden_bias = wide(expand_bias.reshape(FF))
    scaling = 1.0 / math.sqrt(HD)
    positions = jnp.arange(TOK_G, dtype=jnp.int32)
    attention_wide = wide(attention)

    def one_group(carry, inputs):
        rows, cot_rows, group_starts = inputs
        rows_wide = wide(rows)
        unit_one, inverse_one = normalize(rows_wide)
        normed_one = (unit_one * gain_one + shift_one).astype(jnp.bfloat16)
        queries = (jnp.dot(normed_one, attention[0], preferred_element_type=jnp.float32) + query_bias).astype(jnp.bfloat16)
        key_rows = jnp.dot(normed_one, attention[1], preferred_element_type=jnp.float32).astype(jnp.bfloat16)
        value_rows = (jnp.dot(normed_one, attention[2], preferred_element_type=jnp.float32) + value_bias).astype(jnp.bfloat16)
        queries3 = wide(queries).reshape(TOK_G, H, HD)
        keys3 = wide(key_rows).reshape(TOK_G, H, HD)
        values3 = wide(value_rows).reshape(TOK_G, H, HD)
        visibility = (positions[None, :] >= group_starts[:, None]) & (positions[None, :] <= positions[:, None])
        scores = jnp.einsum('qhd,khd->hqk', queries3, keys3, precision=HIGHEST_PRECISION) * scaling
        scores = jnp.where(visibility[None], scores, -jnp.inf)
        row_peak = lax.optimization_barrier(jnp.max(scores, axis=-1, keepdims=True))
        logsum = row_peak + jnp.log(lax.optimization_barrier(jnp.sum(jnp.exp(scores - row_peak), axis=-1, keepdims=True)))
        probability = jnp.exp(scores - logsum)
        prob_half = probability.astype(jnp.bfloat16)
        context = jnp.einsum('hqk,khd->qhd', wide(prob_half), values3, precision=HIGHEST_PRECISION).reshape(TOK_G, D).astype(jnp.bfloat16)
        residual = rows_wide + (jnp.dot(context, combine, preferred_element_type=jnp.float32) + bias_combine)
        unit_two, inverse_two = normalize(residual)
        normed_two = (unit_two * gain_two + shift_two).astype(jnp.bfloat16)
        hidden = jnp.dot(normed_two, expand, preferred_element_type=jnp.float32) + hidden_bias
        activated_wide, gelu_pull = jax.vjp(gelu_tanh, hidden)
        activated = activated_wide.astype(jnp.bfloat16)
        mixed = jnp.dot(activated, contract, preferred_element_type=jnp.float32) + bias_contract
        output = residual + mixed
        cot_wide = wide(cot_rows)
        contract_g = jnp.dot(activated.T, cot_rows, preferred_element_type=jnp.float32)
        conbias_g = lax.optimization_barrier(jnp.sum(cot_wide, axis=0))
        grad_hidden = gelu_pull(jnp.dot(cot_rows, contract.T, preferred_element_type=jnp.float32))[0]
        expbias_g = lax.optimization_barrier(jnp.sum(grad_hidden, axis=0))
        grad_hidden_half = grad_hidden.astype(jnp.bfloat16)
        expand_g = jnp.dot(normed_two.T, grad_hidden_half, preferred_element_type=jnp.float32)
        grad_normed_two = jnp.dot(grad_hidden_half, expand.T, preferred_element_type=jnp.float32)
        grad_residual = cot_wide + normalize_back(grad_normed_two, unit_two, inverse_two, gain_two)
        secondgain_g = lax.optimization_barrier(jnp.sum(grad_normed_two * unit_two, axis=0))
        secondshift_g = lax.optimization_barrier(jnp.sum(grad_normed_two, axis=0))
        combias_g = lax.optimization_barrier(jnp.sum(grad_residual, axis=0))
        grad_residual_half = grad_residual.astype(jnp.bfloat16)
        combine_g = jnp.dot(context.T, grad_residual_half, preferred_element_type=jnp.float32)
        grad_context = jnp.dot(grad_residual_half, combine.T, preferred_element_type=jnp.float32).astype(jnp.bfloat16)
        grad_context3 = wide(grad_context).reshape(TOK_G, H, HD)
        context3 = wide(context).reshape(TOK_G, H, HD)
        grad_prob = jnp.einsum('qhd,khd->hqk', grad_context3, values3, precision=HIGHEST_PRECISION)
        correction = jnp.einsum('qhd,qhd->hq', grad_context3, context3, precision=HIGHEST_PRECISION)
        grad_scores = rounded(probability * (grad_prob - correction[..., None]) * scaling)
        grad_queries = jnp.einsum('hqk,khd->qhd', grad_scores, keys3, precision=HIGHEST_PRECISION).reshape(TOK_G, D)
        grad_keys = jnp.einsum('hqk,qhd->khd', grad_scores, queries3, precision=HIGHEST_PRECISION).reshape(TOK_G, D)
        grad_values = jnp.einsum('hqk,qhd->khd', wide(prob_half), grad_context3, precision=HIGHEST_PRECISION).reshape(TOK_G, D)
        attbias_g = jnp.stack([lax.optimization_barrier(jnp.sum(grad_queries, axis=0)), lax.optimization_barrier(jnp.sum(grad_values, axis=0))]).reshape(2, H, HD)
        grad_parts = jnp.stack([grad_queries, grad_keys, grad_values]).astype(jnp.bfloat16)
        attention_g = jnp.einsum('gd,pgc->pdc', wide(normed_one), wide(grad_parts), precision=HIGHEST_PRECISION)
        grad_normed_one = jnp.einsum('pgc,pdc->gd', wide(grad_parts), attention_wide, precision=HIGHEST_PRECISION)
        tokens_g = grad_residual + normalize_back(grad_normed_one, unit_one, inverse_one, gain_one)
        firstgain_g = lax.optimization_barrier(jnp.sum(grad_normed_one * unit_one, axis=0))
        firstshift_g = lax.optimization_barrier(jnp.sum(grad_normed_one, axis=0))
        terms = (firstgain_g, firstshift_g, attention_g, attbias_g, combine_g, combias_g, secondgain_g, secondshift_g, expand_g, expbias_g.reshape(H, FF // H), contract_g, conbias_g)
        carry = tuple((total + term for total, term in zip(carry, terms)))
        return (carry, (output, tokens_g))
    initial = (jnp.zeros((D,), jnp.float32), jnp.zeros((D,), jnp.float32), jnp.zeros((3, D, D), jnp.float32), jnp.zeros((2, H, HD), jnp.float32), jnp.zeros((D, D), jnp.float32), jnp.zeros((D,), jnp.float32), jnp.zeros((D,), jnp.float32), jnp.zeros((D,), jnp.float32), jnp.zeros((D, FF), jnp.float32), jnp.zeros((H, FF // H), jnp.float32), jnp.zeros((FF, D), jnp.float32), jnp.zeros((D,), jnp.float32))
    final, (outputs, token_grads) = lax.scan(one_group, initial, (tokens.reshape(groups, TOK_G, D), cotangent.reshape(groups, TOK_G, D), starts.reshape(groups, TOK_G)))
    firstgain_grad, firstshift_grad, attention_grad, attenbias_grad, combine_grad, combias_grad, secondgain_grad, secondshift_grad, expand_grad, expbias_grad, contract_grad, conbias_grad = final
    return (outputs.reshape(TOKENS, D), token_grads.reshape(TOKENS, D), firstgain_grad, firstshift_grad, attention_grad, attenbias_grad, combine_grad, combias_grad, secondgain_grad, secondshift_grad, expand_grad, expbias_grad, contract_grad, conbias_grad)
```

```python
import math

import jax
import jax.numpy as jnp
from jax import lax
from jax.sharding import PartitionSpec as P

H = 16
HD = 64
FF = 4096


EPSILON = 1e-05
SQRT_TWO_PI = 0.7978845608028654
CUBIC = 0.044715
BLOCK_ROWS = 512


def normalize(values):
    center = values - jnp.mean(values, axis=-1, keepdims=True)
    inverse = lax.rsqrt(jnp.mean(center * center, axis=-1, keepdims=True) + EPSILON)
    return (center * inverse, inverse)


def normalize_back(upstream, unit_rows, inverse, gain):
    scaled = upstream * gain
    return inverse * (
        scaled
        - jnp.mean(scaled, axis=-1, keepdims=True)
        - unit_rows * jnp.mean(scaled * unit_rows, axis=-1, keepdims=True)
    )


def gelu_tanh(hidden):
    return (
        0.5 * hidden * (1.0 + jnp.tanh(SQRT_TWO_PI * (hidden + CUBIC * hidden * hidden * hidden)))
    )


def visible(starts, offset, rows_block):
    row_index = offset + jnp.arange(rows_block, dtype=jnp.int32)
    col_index = jnp.arange(starts.shape[0], dtype=jnp.int32)
    row_start = starts[offset : offset + rows_block]
    return (col_index[None, :] >= row_start[:, None]) & (col_index[None, :] <= row_index[:, None])


def block_scores(queries3, keys3, starts, offset, rows_block, scaling):
    span = offset + rows_block
    scores = (
        jnp.einsum(
            "qhd,khd->hqk",
            queries3[offset:span],
            keys3[:span],
            preferred_element_type=jnp.float32,
        )
        * scaling
    )
    seen = visible(starts, offset, rows_block)[:, :span]
    return jnp.where(seen[None], scores, -jnp.inf)


def attend_forward(queries3, keys3, values3, starts, offset, rows_block):
    scaling = 1.0 / math.sqrt(HD)
    span = offset + rows_block
    scores = block_scores(queries3, keys3, starts, offset, rows_block, scaling)
    row_peak = jnp.max(scores, axis=-1, keepdims=True)
    logsum = row_peak + jnp.log(jnp.sum(jnp.exp(scores - row_peak), axis=-1, keepdims=True))
    weights = jnp.exp(scores - logsum).astype(jnp.bfloat16)
    context = jnp.einsum(
        "hqk,khd->qhd", weights, values3[:span], preferred_element_type=jnp.float32
    )
    return context.astype(jnp.bfloat16).reshape(rows_block, -1), logsum


def attend_backward(queries3, keys3, values3, context3, grad3, logsums, starts):
    length = queries3.shape[0]
    scaling = 1.0 / math.sqrt(HD)
    rows_block = min(BLOCK_ROWS, length)
    grad_keys = 0.0
    grad_values = 0.0
    grad_blocks = []
    for place, offset in enumerate(range(0, length, rows_block)):
        span = offset + rows_block
        scores = block_scores(queries3, keys3, starts, offset, rows_block, scaling)
        probability = jnp.exp(scores - logsums[place])
        prob_half = probability.astype(jnp.bfloat16)
        grad_here = grad3[offset:span]
        grad_prob = jnp.einsum(
            "qhd,khd->hqk", grad_here, values3[:span], preferred_element_type=jnp.float32
        )
        correction = jnp.einsum(
            "qhd,qhd->hq",
            grad_here.astype(jnp.float32),
            context3[offset:span].astype(jnp.float32),
        )
        grad_scores = (probability * (grad_prob - correction[..., None]) * scaling).astype(
            jnp.bfloat16
        )
        grad_blocks.append(
            jnp.einsum("hqk,khd->qhd", grad_scores, keys3[:span], preferred_element_type=jnp.float32)
        )
        beyond = ((0, length - span), (0, 0), (0, 0))
        grad_keys = grad_keys + jnp.pad(
            jnp.einsum(
                "hqk,qhd->khd",
                grad_scores,
                queries3[offset:span],
                preferred_element_type=jnp.float32,
            ),
            beyond,
        )
        grad_values = grad_values + jnp.pad(
            jnp.einsum("hqk,qhd->khd", prob_half, grad_here, preferred_element_type=jnp.float32),
            beyond,
        )
    return (
        jnp.concatenate(grad_blocks, axis=0).reshape(length, -1),
        grad_keys.reshape(length, -1),
        grad_values.reshape(length, -1),
    )


SWAP = ((0, 1), (1, 0))


def swap(rows):
    return lax.ppermute(rows, "tensor", SWAP)


def own_rows(rows, count, position):
    return lax.dynamic_slice_in_dim(rows, position * count, count, axis=0)


def gather_rows(rows, parts, position):
    if parts != 2:
        return lax.all_gather(rows, "tensor", axis=0, tiled=True)
    other = swap(rows)
    low = position == 0
    return jnp.concatenate([jnp.where(low, rows, other), jnp.where(low, other, rows)], axis=0)


def sum_full(partial, parts):
    if parts != 2:
        return lax.psum(partial.astype(jnp.bfloat16), "tensor").astype(jnp.float32)
    return partial + swap(partial.astype(jnp.bfloat16)).astype(jnp.float32)


def sum_own(partial, parts, position):
    if parts != 2:
        return lax.psum_scatter(
            partial.astype(jnp.bfloat16), "tensor", scatter_dimension=0, tiled=True
        ).astype(jnp.float32)
    count = partial.shape[0] // 2
    sent = own_rows(partial.astype(jnp.bfloat16), count, 1 - position)
    return own_rows(partial, count, position) + swap(sent).astype(jnp.float32)


def gather_weight(shard):
    return lax.all_gather(shard, "dp", axis=0, tiled=True)


def scatter_grad(grad):
    return lax.psum_scatter(
        grad.astype(jnp.bfloat16), "dp", scatter_dimension=0, tiled=True
    ).astype(jnp.float32)


def as_columns(flat, rows):
    short = -flat.shape[-1] % rows
    flat = jnp.pad(flat, [(0, 0)] * (flat.ndim - 1) + [(0, short)])
    return flat.reshape(-1, (flat.shape[-1]) // rows)


def local(
    tokens,
    cotangent,
    starts,
    first_gain,
    first_shift,
    attention,
    attention_bias,
    combine,
    combine_bias,
    second_gain,
    second_shift,
    expand,
    expand_bias,
    contract,
    contract_bias,
):
    parts = lax.axis_size("tensor")
    position = lax.axis_index("tensor")
    groups = lax.axis_size("dp")
    own_count = tokens.shape[0]
    length = own_count * parts
    shard_rows = first_gain.shape[0]
    columns = attention.shape[2]
    heads_here = columns // HD
    half = jnp.bfloat16

    vectors = jnp.stack(
        [first_gain, first_shift, combine_bias, second_gain, second_shift, contract_bias], axis=1
    )
    bias_flat = jnp.concatenate([attention_bias.reshape(-1), expand_bias.reshape(-1)])
    packed = jnp.concatenate(
        [
            attention.transpose(1, 0, 2).reshape(shard_rows, 3 * columns),
            vectors,
            as_columns(bias_flat, shard_rows),
        ],
        axis=1,
    )
    packed = jnp.pad(packed, ((0, 0), (0, -packed.shape[1] % 128)))
    rows_tokens = gather_rows(tokens, parts, position)
    full_packed = gather_weight(packed)
    full_combine = gather_weight(combine.T)
    full_expand = gather_weight(expand)
    full_contract = gather_weight(contract.T)
    rows_cot = gather_rows(cotangent, parts, position)

    full_attention = full_packed[:, : 3 * columns]
    extra = full_packed[:, 3 * columns :]
    gain_one, shift_one, bias_combine, gain_two, shift_two, bias_contract = (
        extra[:, :6].T.astype(jnp.float32)
    )
    bias_cols = -(-bias_flat.shape[0] // shard_rows)
    bias_rows = extra[:, 6 : 6 + bias_cols].reshape(groups, -1).astype(jnp.float32)
    att_count = attention_bias.size
    heads_bias = (
        bias_rows[:, :att_count]
        .reshape((groups,) + attention_bias.shape)
        .transpose(1, 2, 0, 3)
        .reshape(2, columns)
    )
    hidden_bias = (
        bias_rows[:, att_count : bias_flat.shape[0]]
        .reshape((groups,) + expand_bias.shape)
        .transpose(1, 0, 2)
        .reshape(-1)
    )

    tokens_wide = rows_tokens.astype(jnp.float32)
    unit_one, inverse_one = normalize(tokens_wide)
    rows_one = (unit_one * gain_one + shift_one).astype(half)
    projected = jnp.dot(rows_one, full_attention, preferred_element_type=jnp.float32)
    queries3 = (projected[:, :columns] + heads_bias[0]).astype(half)
    keys3 = projected[:, columns : 2 * columns].astype(half)
    values3 = (projected[:, 2 * columns :] + heads_bias[1]).astype(half)
    queries3, keys3, values3 = (
        member.reshape(length, heads_here, HD) for member in (queries3, keys3, values3)
    )
    rows_block = min(BLOCK_ROWS, length)
    contexts, logsums, attended = [], [], []
    for offset in range(0, length, rows_block):
        context, logsum = attend_forward(queries3, keys3, values3, starts, offset, rows_block)
        contexts.append(context)
        logsums.append(logsum)
        attended.append(
            sum_full(
                jnp.einsum("tc,dc->td", context, full_combine, preferred_element_type=jnp.float32),
                parts,
            )
        )
    context = jnp.concatenate(contexts, axis=0)
    grad_act = jnp.einsum("td,df->tf", rows_cot, full_contract, preferred_element_type=jnp.float32)
    residual = tokens_wide + (jnp.concatenate(attended, axis=0) + bias_combine)
    unit_two, inverse_two = normalize(residual)
    rows_two = (unit_two * gain_two + shift_two).astype(half)
    hidden = jnp.dot(rows_two, full_expand, preferred_element_type=jnp.float32) + hidden_bias
    activated, gelu_pull = jax.vjp(gelu_tanh, hidden)
    activated = activated.astype(half)
    grad_hidden = gelu_pull(grad_act)[0]
    expbias_grad = jnp.sum(grad_hidden, axis=0)
    grad_hidden_half = grad_hidden.astype(half)
    grad_two = []
    for offset in range(0, length, rows_block):
        grad_two.append(
            sum_full(
                jnp.einsum(
                    "tf,df->td",
                    grad_hidden_half[offset : offset + rows_block],
                    full_expand,
                    preferred_element_type=jnp.float32,
                ),
                parts,
            )
        )
    grad_normed_two = jnp.concatenate(grad_two, axis=0)
    contract_grad = scatter_grad(
        jnp.einsum("td,tf->df", rows_cot, activated, preferred_element_type=jnp.float32)
    )
    expand_grad = scatter_grad(
        jnp.einsum("td,tf->df", rows_two, grad_hidden_half, preferred_element_type=jnp.float32)
    )
    mixed = sum_own(
        jnp.einsum("tf,df->td", activated, full_contract, preferred_element_type=jnp.float32),
        parts,
        position,
    )
    result = own_rows(residual, own_count, position) + (mixed + bias_contract)

    cot_wide = rows_cot.astype(jnp.float32)
    grad_residual = cot_wide + normalize_back(grad_normed_two, unit_two, inverse_two, gain_two)
    grad_res_half = grad_residual.astype(half)
    combine_grad = scatter_grad(
        jnp.einsum("td,tc->dc", grad_res_half, context, preferred_element_type=jnp.float32)
    )
    grad_context = jnp.einsum(
        "td,dc->tc", grad_res_half, full_combine, preferred_element_type=jnp.float32
    ).astype(half)
    grad_queries, grad_keys, grad_values = attend_backward(
        queries3,
        keys3,
        values3,
        context.reshape(length, heads_here, HD),
        grad_context.reshape(length, heads_here, HD),
        logsums,
        starts,
    )
    attbias_grad = jnp.stack([jnp.sum(grad_queries, axis=0), jnp.sum(grad_values, axis=0)])
    grad_parts = jnp.concatenate([grad_queries, grad_keys, grad_values], axis=1).astype(half)
    grad_normed_one = sum_own(
        jnp.einsum("tc,dc->td", grad_parts, full_attention, preferred_element_type=jnp.float32),
        parts,
        position,
    )
    attention_grad = jnp.einsum(
        "td,tc->dc", rows_one, grad_parts, preferred_element_type=jnp.float32
    )
    unit_own = own_rows(unit_one, own_count, position)
    tokens_grad = own_rows(grad_residual, own_count, position) + normalize_back(
        grad_normed_one, unit_own, own_rows(inverse_one, own_count, position), gain_one
    )
    vector_grads = jnp.stack(
        [
            jnp.sum(grad_normed_one * unit_own, axis=0),
            jnp.sum(grad_normed_one, axis=0),
            jnp.sum(grad_residual, axis=0),
            jnp.sum(grad_normed_two * unit_two, axis=0),
            jnp.sum(grad_normed_two, axis=0),
            jnp.sum(cot_wide, axis=0),
        ],
        axis=1,
    )
    att_shape = attention_bias.shape
    exp_shape = expand_bias.shape
    bias_grads = jnp.concatenate(
        [
            attbias_grad.reshape(2, heads_here, groups, att_shape[2])
            .transpose(2, 0, 1, 3)
            .reshape(groups, -1),
            expbias_grad.reshape(exp_shape[0], groups, exp_shape[1])
            .transpose(1, 0, 2)
            .reshape(groups, -1),
        ],
        axis=1,
    )
    small_grads = jnp.concatenate([vector_grads, as_columns(bias_grads, shard_rows)], axis=1)
    small_grads = jnp.pad(small_grads, ((0, 0), (0, -small_grads.shape[1] % 128)))
    summed = scatter_grad(jnp.concatenate([attention_grad, small_grads], axis=1))
    attention_grad = summed[:, : 3 * columns].reshape(shard_rows, 3, columns).transpose(1, 0, 2)
    small = summed[:, 3 * columns :]
    paired = small[:, :2]
    paired = paired + swap(paired) if parts == 2 else lax.psum(paired, "tensor")
    spread = jnp.concatenate([paired, small[:, 2:6]], axis=1).T
    share = shard_rows // parts
    spread = lax.dynamic_slice_in_dim(spread, position * share, share, axis=1)
    flat = small[:, 6 : 6 + bias_cols].reshape(-1)
    return (
        result,
        tokens_grad,
        spread[0],
        spread[1],
        attention_grad,
        flat[:att_count].reshape(att_shape),
        combine_grad.T,
        spread[2],
        spread[3],
        spread[4],
        expand_grad,
        flat[att_count : bias_flat.shape[0]].reshape(exp_shape),
        contract_grad.T,
        spread[5],
    )


def solution(mesh):
    in_specs = (
        P(("dp", "tensor"), None),
        P(("dp", "tensor"), None),
        P("dp"),
        P("dp"),
        P("dp"),
        P(None, "dp", "tensor"),
        P(None, "tensor", "dp"),
        P("tensor", "dp"),
        P("dp"),
        P("dp"),
        P("dp"),
        P("dp", "tensor"),
        P("tensor", "dp"),
        P("tensor", "dp"),
        P("dp"),
    )
    out_specs = (
        P(("dp", "tensor"), None),
        P(("dp", "tensor"), None),
        P(("dp", "tensor")),
        P(("dp", "tensor")),
        P(None, "dp", "tensor"),
        P(None, "tensor", "dp"),
        P("tensor", "dp"),
        P(("dp", "tensor")),
        P(("dp", "tensor")),
        P(("dp", "tensor")),
        P("dp", "tensor"),
        P("tensor", "dp"),
        P("tensor", "dp"),
        P(("dp", "tensor")),
    )
    return jax.shard_map(local, mesh=mesh, in_specs=in_specs, out_specs=out_specs, check_vma=False)
```
